32 devices in a mesh: grp: 2 (over y), ctx: 4 (over z), head: 2 (over x), sub: 2 (over core).
Axes of the slice: x: 2, y: 2, z: 4, core: 2. Of those that a mesh axis runs over, the one named last changes fastest.
Arguments:
- queries: bfloat16 [1024, 8192], P(('grp', 'ctx'), 'head'), parts along dimension 0, may hold values from -120 to 120
- stretch_keys: bfloat16 [1024, 1024], P(('grp', 'ctx', 'sub'), 'head'), parts along dimension 0, may hold values from -6 to 6
- stretch_values: bfloat16 [1024, 1024], P(('grp', 'ctx', 'sub'), 'head'), parts along dimension 0, may hold values from -6 to 6
- cache_keys: bfloat16 [3072, 1024], P(('grp', 'ctx', 'sub'), 'head'), parts along dimension 0, may hold values from -6 to 6
- cache_values: bfloat16 [3072, 1024], P(('grp', 'ctx', 'sub'), 'head'), parts along dimension 0, may hold values from -6 to 6
- doc_lengths: int32 [24], P('grp'), parts along dimension 0, may hold values from 1 to 256, 2048 in all
Outputs:
- attended: bfloat16 [1024, 8192], P(('grp', 'ctx'), ('head', 'sub')), parts along dimension 0
The draws below stay inside these ranges and needn't reach their ends.
There are 2 independent parts, one for each index of `grp`. The reference program is written for one: setup_inputs(seed, part) draws one part's arguments, and reference() takes and returns one part's arrays. A program takes and returns all parts, laid end to end along the dimension named above; each array names one. Nothing has to cross between parts.
Inputs may be any that keep to these rules, and one draw needn't show every extreme that they name: `doc_lengths`: the 12 documents fill all 2048 positions in order, none longer than 256 tokens and one exactly 256.
All inputs are finite; a program needn't handle non-finite values.
Results may differ from the reference program's by a relative error of at most 0.013.
Values may be sent and summed in bfloat16 or wider, within the bound.
A program may use at most 64 MiB of HBM per device.

```python
import math
import jax
import jax.numpy as jnp
import numpy as np
from jax import lax

Q_HEADS = 64
KV_HEADS = 8
HEAD_DIM = 128
NDOC = 12
STRETCH = 512
PREFIX = 1536
DOCMAX = 256


def key_base(key):
    return jnp.clip(jax.random.normal(jax.random.fold_in(key, 7101), (STRETCH, KV_HEADS * HEAD_DIM), jnp.float32), -4.5, 4.5)


def draw_stretch_keys(key, part):
    base = key_base(key)
    return base.astype(jnp.bfloat16)


def draw_queries(key, part):
    values = jnp.clip(jax.random.normal(jax.random.fold_in(key, 7103), (STRETCH, Q_HEADS * HEAD_DIM), jnp.float32), -4.5, 4.5)
    return values.astype(jnp.bfloat16)


def level_of(stream_key, dims, pieces, low, largest):
    loudness, own = 1.0, jax.random.fold_in(stream_key, 6)
    for axis_at, shards_of in pieces:
        heights = jnp.exp(jax.random.uniform(jax.random.fold_in(own, axis_at), (shards_of,), jnp.float32, low / len(pieces), largest / len(pieces)))
        loudness = loudness * jnp.repeat(heights, dims[axis_at] // shards_of).reshape([-1 if axis == axis_at else 1 for axis in range(len(dims))])
    return loudness


def length_profile(number_of, total, most, skew):
    loads = [(1 << 20) // math.isqrt(standing ** skew) + 1 for standing in range(2, number_of + 1)]
    spare, holding = total - most - (number_of - 1), [1] * (number_of - 1)
    while spare > 0:
        candidates = [i for i in range(number_of - 1) if holding[i] < most]
        pool, left = sum([loads[i] for i in candidates]), spare
        for i in candidates:
            more = min(most - holding[i], max(1, left * loads[i] // pool), spare)
            holding[i] = holding[i] + more
            spare = spare - more
    return np.array([most] + holding)


def uneven_parts(stream_key, count, total, reach, slope):
    if count == 2:
        one = jax.random.randint(stream_key, (), max(1, total - reach), min(reach, total - 1) + 1)
        return jnp.stack([one, total - one])
    lengths = jnp.asarray(length_profile(count, total, reach, slope), jnp.int32)
    twos = (count - 1) // 2
    source_of, sink = lengths[1:1 + 2 * twos:2], lengths[2:2 + 2 * twos:2]
    slack = jnp.minimum(source_of - 1, reach - sink)
    shifted = jax.random.randint(jax.random.fold_in(stream_key, 1), (twos,), 0, 1 << 20) % (slack + 1)
    lengths = lengths.at[1:1 + 2 * twos:2].set(source_of - shifted).at[2:2 + 2 * twos:2].set(sink + shifted)
    return lengths[jax.random.permutation(jax.random.fold_in(stream_key, 2), count)]


def bell_draw(own_key, shape, scale, limit, split=(), kind=jnp.bfloat16):
    entries = scale * jax.random.normal(own_key, shape, jnp.float32)
    if split:
        entries = entries * level_of(own_key, shape, split, -0.22, 0.18)
    return jnp.clip(entries, -limit, limit).astype(kind)


def setup_inputs(seed: int = 0, part: int = 0) -> dict:
    seeds = jax.random.split(jax.random.key(seed), 7)
    own_keys = jax.random.split(jax.random.fold_in(seeds[6], part), 7)
    queries = draw_queries(jax.random.fold_in(jax.random.fold_in(seeds[6], part), 71), part)
    stretch_keys = draw_stretch_keys(jax.random.fold_in(jax.random.fold_in(seeds[6], part), 71), part)
    stretch_values = bell_draw(own_keys[2], (STRETCH, KV_HEADS * HEAD_DIM), 1.0, 6.0, ((0, 8), (1, 2)))
    cache_keys = bell_draw(own_keys[3], (PREFIX, KV_HEADS * HEAD_DIM), 1.0, 6.0, ((0, 8), (1, 2)))
    cache_values = bell_draw(own_keys[4], (PREFIX, KV_HEADS * HEAD_DIM), 1.0, 6.0, ((0, 8), (1, 2)))
    doc_lengths = uneven_parts(own_keys[5], NDOC, PREFIX + STRETCH, DOCMAX, 2).astype(jnp.int32)
    return {"queries": queries, "stretch_keys": stretch_keys, "stretch_values": stretch_values, "cache_keys": cache_keys, "cache_values": cache_values, "doc_lengths": doc_lengths}


NEG_FILL = -1.0e30


def reference(queries, stretch_keys, stretch_values, cache_keys, cache_values, doc_lengths):
    prefix_len = cache_keys.shape[0]
    stretch_len = stretch_keys.shape[0]
    keys_all = jnp.concatenate([cache_keys, stretch_keys], axis=0)
    values_all = jnp.concatenate([cache_values, stretch_values], axis=0)
    doc_ends = jnp.cumsum(doc_lengths).astype(jnp.int32)
    positions = jnp.arange(prefix_len + stretch_len, dtype=jnp.int32)
    doc_index = jnp.sum((positions[:, None] >= doc_ends[None, :]).astype(jnp.int32), axis=1).astype(jnp.int32)
    group_size = Q_HEADS // KV_HEADS
    query_block = math.gcd(stretch_len, 512)
    window = DOCMAX + query_block
    score_scale = HEAD_DIM ** -0.5

    def one_block(block_index):
        query_first = (block_index * query_block).astype(jnp.int32)
        query_start = (prefix_len + query_first).astype(jnp.int32)
        key_start = (query_start - DOCMAX).astype(jnp.int32)
        query_rows = lax.dynamic_slice_in_dim(queries, query_first, query_block, 0)
        key_rows = lax.dynamic_slice_in_dim(keys_all, key_start, window, 0)
        value_rows = lax.dynamic_slice_in_dim(values_all, key_start, window, 0)
        query_pos = query_start + jnp.arange(query_block, dtype=jnp.int32)
        key_pos = key_start + jnp.arange(window, dtype=jnp.int32)
        query_doc = lax.dynamic_slice_in_dim(doc_index, query_start, query_block, 0)
        key_doc = lax.dynamic_slice_in_dim(doc_index, key_start, window, 0)
        allowed = (key_doc[None, :] == query_doc[:, None]) & (key_pos[None, :] <= query_pos[:, None])
        query_heads = query_rows.astype(jnp.float32).reshape(query_block, KV_HEADS, group_size, HEAD_DIM)
        key_heads = key_rows.astype(jnp.float32).reshape(window, KV_HEADS, HEAD_DIM)
        value_heads = value_rows.astype(jnp.float32).reshape(window, KV_HEADS, HEAD_DIM)
        scores = jnp.einsum("tgjd,kgd->gjtk", query_heads, key_heads) * score_scale
        scores = jnp.where(allowed, scores, NEG_FILL)
        row_max = jnp.max(scores, axis=3, keepdims=True)
        weights = jnp.where(allowed, jnp.exp(scores - row_max), 0.0)
        row_sum = jnp.sum(weights, axis=3)
        rounded = lax.optimization_barrier(weights.astype(jnp.bfloat16))
        rounded = rounded.astype(jnp.float32)
        weighted = jnp.einsum("gjtk,kgd->tgjd", rounded, value_heads)
        normed = weighted / jnp.transpose(row_sum, (2, 0, 1))[..., None]
        return normed.reshape(query_block, Q_HEADS * HEAD_DIM).astype(jnp.bfloat16)

    outputs = lax.map(one_block, jnp.arange(stretch_len // query_block, dtype=jnp.int32))
    return outputs.reshape(stretch_len, Q_HEADS * HEAD_DIM)
```

```python
import functools

import jax
import jax.numpy as jnp
from jax import lax
from jax.experimental import pallas as pl
from jax.experimental.pallas import tpu as pltpu
from jax.sharding import PartitionSpec as P

HEAD_DIM = 128
NEG_FILL = -1e30
LOG2_E = 1.4426950408889634


def kernel(
    n_ctx,
    n_sub,
    q_hbm,
    sk_hbm,
    sv_hbm,
    ck_hbm,
    cv_hbm,
    docs_hbm,
    out_ref,
    q_v,
    k_buf,
    v_buf,
    docs,
    max_v,
    sum_v,
    acc_v,
    part_v,
    q_sem,
    docs_sem,
    own_sem,
    pair_send,
    cache_send,
    relay_send,
    recv_sem,
    pair_sem,
):
    ctx = lax.axis_index("ctx")
    sub = lax.axis_index("sub")
    other = n_sub - 1 - sub
    flat = ctx * n_sub + sub
    rows = q_hbm.shape[0]
    unit = sk_hbm.shape[0]
    all_groups = sk_hbm.shape[1] // HEAD_DIM
    groups = max(1, all_groups // n_sub)
    cols = groups * HEAD_DIM
    heads = q_hbm.shape[1] // HEAD_DIM // n_sub
    per_group = heads // groups
    per_cache = ck_hbm.shape[0] // unit
    prefix_units = per_cache * n_sub * n_ctx
    reach = n_ctx // 2
    back = reach * n_sub
    ndoc = docs_hbm.shape[0]
    scale = HEAD_DIM**-0.5 * LOG2_E

    def remote(src, dst, send, recv, to_ctx, to_sub):
        return pltpu.make_async_remote_copy(
            src_ref=src,
            dst_ref=dst,
            send_sem=send,
            recv_sem=recv,
            device_id={"ctx": to_ctx, "sub": to_sub},
            device_id_type=pl.DeviceIdType.MESH,
        )

    def slot(buf, k):
        start = k * unit
        if not isinstance(k, int):
            start = pl.multiple_of(start, unit)
        return buf.at[pl.ds(start, unit), :]

    def columns(to_sub):
        start = to_sub * all_groups // n_sub * HEAD_DIM
        if not isinstance(start, int):
            start = pl.multiple_of(start, HEAD_DIM)
        return pl.ds(start, cols)

    bufs = (k_buf, v_buf)
    stretch = (sk_hbm, sv_hbm)
    cache = (ck_hbm, cv_hbm)

    barrier = pltpu.get_barrier_semaphore()

    def greet(to_ctx, to_sub):
        pl.semaphore_signal(
            barrier,
            inc=1,
            device_id={"ctx": to_ctx, "sub": to_sub},
            device_id_type=pl.DeviceIdType.MESH,
        )

    first_owner = (prefix_units - back) // (per_cache * n_sub)

    @pl.when(ctx == 0)
    def _():
        for source in range(first_owner, n_ctx):
            greet(source, sub)

    @pl.when(ctx >= 1)
    def _():
        greet(ctx - 1, sub)

    docs_copy = pltpu.make_async_copy(docs_hbm, docs, docs_sem)
    docs_copy.start()
    q_copies = []
    for h in range(heads):
        at = pl.multiple_of((sub * heads + h) * HEAD_DIM, HEAD_DIM)
        copy = pltpu.make_async_copy(
            q_hbm.at[:, pl.ds(at, HEAD_DIM)],
            q_v.at[pl.ds(h * rows, rows), :],
            q_sem.at[h],
        )
        copy.start()
        q_copies.append(copy)
    own_copies = []
    for i in range(2):
        copy = pltpu.make_async_copy(
            stretch[i].at[:, columns(sub)],
            slot(bufs[i], back + sub),
            own_sem.at[i],
        )
        copy.start()
        own_copies.append(copy)

    def offset(j):
        return flat * per_cache + j - (prefix_units - back)

    expected = (
        jnp.where(ctx + 1 < n_ctx, 1, 0)
        + jnp.where(ctx >= first_owner, 1, 0)
        + jnp.where(sub == 0, 1, 0)
    )
    pl.semaphore_wait(barrier, expected)

    @pl.when(sub == 1)
    def _():
        greet(ctx, 0)

    @pl.when(sub == 0)
    def _():
        pl.semaphore_signal(
            pair_sem,
            inc=1,
            device_id={"ctx": ctx, "sub": 1},
            device_id_type=pl.DeviceIdType.MESH,
        )

    def cache_copy(j, t, i):
        to_slot = offset(j)
        return remote(
            cache[i].at[pl.ds(j * unit, unit), columns(t)],
            slot(bufs[i], to_slot),
            cache_send.at[j, t, i],
            recv_sem.at[to_slot, i],
            0,
            t,
        )

    def pair_copy(i):
        return remote(
            stretch[i].at[:, columns(other)],
            slot(bufs[i], back + sub),
            pair_send.at[i],
            recv_sem.at[back + sub, i],
            ctx,
            other,
        )

    def relays(k, i, act):
        @pl.when(ctx + 1 < n_ctx)
        def _():
            act(
                remote(
                    slot(bufs[i], k),
                    slot(bufs[i], k - n_sub),
                    relay_send.at[k, i],
                    recv_sem.at[k - n_sub, i],
                    ctx + 1,
                    sub,
                )
            )

    def send_cache(j, t):
        for i in range(2):
            cache_copy(j, t, i).start()

    @pl.when(sub == 1)
    def _():
        for j in reversed(range(per_cache)):

            @pl.when(offset(j) >= n_sub)
            def _(j=j):
                send_cache(j, 1)

    for i in range(2):
        own_copies[i].wait()
        relays(back + sub, i, lambda copy: copy.start())

    @pl.when(sub == 1)
    def _():
        pl.semaphore_wait(pair_sem, 1)

    for j in range(per_cache):

        @pl.when(offset(j) >= n_sub)
        def _(j=j):
            send_cache(j, 0)

            @pl.when(sub == 0)
            def _():
                send_cache(j, 1)

    for j in range(per_cache):

        @pl.when((offset(j) >= 0) & (offset(j) < n_sub))
        def _(j=j):
            for t in range(n_sub):
                send_cache(j, t)

    for i in range(2):
        pair_copy(i).start()

    def arrived(k, i):
        piece = slot(bufs[i], k)
        remote(piece, piece, relay_send.at[0, i], recv_sem.at[k, i], ctx, sub).wait_recv()

    docs_copy.wait()
    q_pos = rows * ctx + prefix_units * unit + lax.broadcasted_iota(jnp.int32, (1, rows), 1)
    end = jnp.int32(0)
    first = jnp.zeros((1, rows), jnp.int32)
    for e in range(ndoc):
        end = end + docs[e]
        first = jnp.maximum(first, jnp.where(q_pos >= end, end, 0))

    wide = min(2, per_group)
    span = wide * rows

    def attend(distance):
        base = (reach - distance) * rows
        k_pos = (
            rows * (ctx - distance)
            + prefix_units * unit
            + lax.broadcasted_iota(jnp.int32, (rows, rows), 0)
        )
        allowed = k_pos >= first
        if distance == 0:
            allowed = allowed & (k_pos <= q_pos)
        bias = jnp.where(allowed, 0.0, NEG_FILL)
        bias = jnp.concatenate([bias] * wide, axis=1)
        blocks = [
            (g, (g * per_group + b * wide) * rows)
            for g in range(groups)
            for b in range(per_group // wide)
        ]

        def weigh(g, at):
            here = pl.ds(at, span)
            keys = k_buf[pl.ds(base, rows), pl.ds(g * HEAD_DIM, HEAD_DIM)]
            scores = lax.dot_general(
                keys,
                q_v[here, :],
                (((1,), (1,)), ((), ())),
                preferred_element_type=jnp.float32,
            )
            scores = scores + bias
            top = jnp.max(scores, axis=0, keepdims=True)
            if distance > 0:
                before = max_v[:, here]
                top = jnp.maximum(top, before)
            weights = jnp.exp2((scores - top) * scale)
            total = jnp.sum(weights, axis=0, keepdims=True)
            shrink = None
            if distance > 0:
                shrink = jnp.exp2((before - top) * scale)
                total = total + sum_v[:, here] * shrink
            if distance < reach:
                max_v[:, here] = top
            return weights.astype(jnp.bfloat16), total, shrink

        def add(g, at, weights, total, shrink):
            here = pl.ds(at, span)
            values = v_buf[pl.ds(base, rows), pl.ds(g * HEAD_DIM, HEAD_DIM)]
            update = lax.dot_general(
                values,
                weights,
                (((0,), (0,)), ((), ())),
                preferred_element_type=jnp.float32,
            )
            if 0 < distance < reach:
                update = update + acc_v[:, here] * shrink
            if distance < reach:
                sum_v[:, here] = total
                acc_v[:, here] = update
            else:
                result = (acc_v[:, here] + update * total).astype(out_ref.dtype)
                for w in range(wide):
                    piece = result[:, w * rows : (w + 1) * rows]
                    out_at = (at // rows + w) * HEAD_DIM
                    out_ref[:, pl.ds(out_at, HEAD_DIM)] = piece.T

        if distance < reach:
            for g, at in blocks:
                add(g, at, *weigh(g, at))
            return
        take(distance, (0,))
        for g, at in blocks:
            weights, total, shrink = weigh(g, at)
            here = pl.ds(at, span)
            part_v[:, here] = weights
            inverse = 1.0 / total
            sum_v[:, here] = inverse
            acc_v[:, here] = acc_v[:, here] * (shrink * inverse)
        take(distance, (1,))
        for g, at in blocks:
            here = pl.ds(at, span)
            add(g, at, part_v[:, here], sum_v[:, here], None)

    for i in range(2):
        arrived(back + other, i)
        relays(back + other, i, lambda copy: copy.start())
    for copy in q_copies:
        copy.wait()

    attend(0)

    def take(distance, kinds=(0, 1)):
        for r in (sub, other):
            k = back - distance * n_sub + r
            for i in kinds:
                arrived(k, i)
                if distance < reach:
                    relays(k, i, lambda copy: copy.start())

    for distance in range(1, reach + 1):
        if distance < reach:
            take(distance)
        attend(distance)

    for j in range(per_cache):

        @pl.when(offset(j) >= 0)
        def _(j=j):
            for t in range(n_sub):
                for i in range(2):
                    cache_copy(j, t, i).wait_send()

    for i in range(2):
        pair_copy(i).wait_send()
    for k in range(n_sub, back + n_sub):
        for i in range(2):
            relays(k, i, lambda copy: copy.wait_send())


def on_device(queries, stretch_keys, stretch_values, cache_keys, cache_values, doc_lengths):
    n_ctx = lax.axis_size("ctx")
    n_sub = lax.axis_size("sub")
    rows = queries.shape[0]
    unit = stretch_keys.shape[0]
    cols = max(1, stretch_keys.shape[1] // HEAD_DIM // n_sub) * HEAD_DIM
    per_cache = cache_keys.shape[0] // unit
    heads = queries.shape[1] // n_sub // HEAD_DIM
    units = (n_ctx // 2 + 1) * n_sub
    return pl.pallas_call(
        functools.partial(kernel, n_ctx, n_sub),
        out_shape=jax.ShapeDtypeStruct((rows, heads * HEAD_DIM), jnp.bfloat16),
        in_specs=[pl.BlockSpec(memory_space=pltpu.HBM)] * 6,
        out_specs=pl.BlockSpec(memory_space=pltpu.VMEM),
        scratch_shapes=[
            pltpu.VMEM((heads * rows, HEAD_DIM), jnp.bfloat16),
            pltpu.VMEM((units * unit, cols), jnp.bfloat16),
            pltpu.VMEM((units * unit, cols), jnp.bfloat16),
            pltpu.SMEM(doc_lengths.shape, jnp.int32),
            pltpu.VMEM((1, heads * rows), jnp.float32),
            pltpu.VMEM((1, heads * rows), jnp.float32),
            pltpu.VMEM((HEAD_DIM, heads * rows), jnp.float32),
            pltpu.VMEM((rows, heads * rows), jnp.bfloat16),
            pltpu.SemaphoreType.DMA((heads,)),
            pltpu.SemaphoreType.DMA,
            pltpu.SemaphoreType.DMA((2,)),
            pltpu.SemaphoreType.DMA((2,)),
            pltpu.SemaphoreType.DMA((per_cache, n_sub, 2)),
            pltpu.SemaphoreType.DMA((units, 2)),
            pltpu.SemaphoreType.DMA((units, 2)),
            pltpu.SemaphoreType.REGULAR,
        ],
        compiler_params=pltpu.CompilerParams(collective_id=0, has_side_effects=True, vmem_limit_bytes=16 * 1024 * 1024),
        name="attend",
    )(
        *(
            pltpu.with_memory_space_constraint(array, pltpu.HBM)
            for array in (
                queries,
                stretch_keys,
                stretch_values,
                cache_keys,
                cache_values,
                doc_lengths,
            )
        )
    )


def solution(mesh):
    in_specs = (
        P(("grp", "ctx"), "head"),
        P(("grp", "ctx", "sub"), "head"),
        P(("grp", "ctx", "sub"), "head"),
        P(("grp", "ctx", "sub"), "head"),
        P(("grp", "ctx", "sub"), "head"),
        P("grp"),
    )
    out_specs = P(("grp", "ctx"), ("head", "sub"))
    return jax.shard_map(
        on_device, mesh=mesh, in_specs=in_specs, out_specs=out_specs, check_vma=False
    )
```

```python
import functools

import jax
import jax.numpy as jnp
from jax import lax
from jax.experimental import pallas as pl
from jax.experimental.pallas import tpu as pltpu
from jax.sharding import PartitionSpec as P

HEAD_DIM = 128
NEG_FILL = -1e30
LOG2_E = 1.4426950408889634


def kernel(
    n_ctx,
    n_sub,
    q_hbm,
    sk_hbm,
    sv_hbm,
    ck_hbm,
    cv_hbm,
    docs_hbm,
    out_ref,
    q_v,
    k_buf,
    v_buf,
    docs,
    max_v,
    sum_v,
    acc_v,
    part_v,
    done_v,
    q_sem,
    docs_sem,
    own_sem,
    pair_send,
    cache_send,
    relay_send,
    recv_sem,
    pair_sem,
):
    ctx = lax.axis_index("ctx")
    sub = lax.axis_index("sub")
    other = n_sub - 1 - sub
    flat = ctx * n_sub + sub
    rows = q_hbm.shape[0]
    unit = sk_hbm.shape[0]
    all_groups = sk_hbm.shape[1] // HEAD_DIM
    groups = max(1, all_groups // n_sub)
    cols = groups * HEAD_DIM
    heads = q_hbm.shape[1] // HEAD_DIM // n_sub
    per_group = heads // groups
    per_cache = ck_hbm.shape[0] // unit
    prefix_units = per_cache * n_sub * n_ctx
    reach = n_ctx // 2
    back = reach * n_sub
    ndoc = docs_hbm.shape[0]
    scale = HEAD_DIM**-0.5 * LOG2_E

    def remote(src, dst, send, recv, to_ctx, to_sub):
        return pltpu.make_async_remote_copy(
            src_ref=src,
            dst_ref=dst,
            send_sem=send,
            recv_sem=recv,
            device_id={"ctx": to_ctx, "sub": to_sub},
            device_id_type=pl.DeviceIdType.MESH,
        )

    def slot(buf, k):
        start = k * unit
        if not isinstance(k, int):
            start = pl.multiple_of(start, unit)
        return buf.at[pl.ds(start, unit), :]

    def columns(to_sub):
        start = to_sub * all_groups // n_sub * HEAD_DIM
        if not isinstance(start, int):
            start = pl.multiple_of(start, HEAD_DIM)
        return pl.ds(start, cols)

    bufs = (k_buf, v_buf)
    stretch = (sk_hbm, sv_hbm)
    cache = (ck_hbm, cv_hbm)

    barrier = pltpu.get_barrier_semaphore()

    def greet(to_ctx, to_sub):
        pl.semaphore_signal(
            barrier,
            inc=1,
            device_id={"ctx": to_ctx, "sub": to_sub},
            device_id_type=pl.DeviceIdType.MESH,
        )

    first_owner = (prefix_units - back) // (per_cache * n_sub)

    @pl.when(ctx == 0)
    def _():
        for source in range(first_owner, n_ctx):
            greet(source, sub)

    @pl.when(ctx >= 1)
    def _():
        greet(ctx - 1, sub)

    docs_copy = pltpu.make_async_copy(docs_hbm, docs, docs_sem)
    q_copies = []
    for h in range(heads):
        at = pl.multiple_of((sub * heads + h) * HEAD_DIM, HEAD_DIM)
        q_copies.append(
            pltpu.make_async_copy(
                q_hbm.at[:, pl.ds(at, HEAD_DIM)],
                q_v.at[pl.ds(h * rows, rows), :],
                q_sem.at[h],
            )
        )
    own_copies = [
        pltpu.make_async_copy(
            stretch[i].at[:, columns(sub)],
            slot(bufs[i], back + sub),
            own_sem.at[i],
        )
        for i in range(2)
    ]

    def fetch():
        for copy in [*own_copies, docs_copy, *q_copies]:
            copy.start()

    @pl.when(ctx < first_owner)
    def _():
        fetch()

    def offset(j):
        return flat * per_cache + j - (prefix_units - back)

    expected = (
        jnp.where(ctx + 1 < n_ctx, 1, 0)
        + jnp.where(ctx >= first_owner, 1, 0)
        + jnp.where(sub == 0, 1, 0)
    )
    pl.semaphore_wait(barrier, expected)

    @pl.when(sub == 1)
    def _():
        greet(ctx, 0)

    @pl.when(sub == 0)
    def _():
        pl.semaphore_signal(
            pair_sem,
            inc=1,
            device_id={"ctx": ctx, "sub": 1},
            device_id_type=pl.DeviceIdType.MESH,
        )

    def cache_copy(j, t, i):
        to_slot = offset(j)
        return remote(
            cache[i].at[pl.ds(j * unit, unit), columns(t)],
            slot(bufs[i], to_slot),
            cache_send.at[j, t, i],
            recv_sem.at[to_slot, i],
            0,
            t,
        )

    def pair_copy(i):
        return remote(
            stretch[i].at[:, columns(other)],
            slot(bufs[i], back + sub),
            pair_send.at[i],
            recv_sem.at[back + sub, i],
            ctx,
            other,
        )

    def relays(k, i, act):
        @pl.when(ctx + 1 < n_ctx)
        def _():
            act(
                remote(
                    slot(bufs[i], k),
                    slot(bufs[i], k - n_sub),
                    relay_send.at[k, i],
                    recv_sem.at[k - n_sub, i],
                    ctx + 1,
                    sub,
                )
            )

    def send_cache(j, t):
        for i in range(2):
            cache_copy(j, t, i).start()

    @pl.when(sub == 1)
    def _():
        for j in reversed(range(per_cache)):

            @pl.when(offset(j) >= n_sub)
            def _(j=j):
                send_cache(j, 1)

    @pl.when(ctx >= first_owner)
    def _():
        fetch()

    for i in range(2):
        own_copies[i].wait()
        relays(back + sub, i, lambda copy: copy.start())

    @pl.when(sub == 1)
    def _():
        pl.semaphore_wait(pair_sem, 1)

    for j in range(per_cache):

        @pl.when(offset(j) >= n_sub)
        def _(j=j):
            send_cache(j, 0)

            @pl.when(sub == 0)
            def _():
                send_cache(j, 1)

    for j in range(per_cache):

        @pl.when((offset(j) >= 0) & (offset(j) < n_sub))
        def _(j=j):
            for t in range(n_sub):
                send_cache(j, t)

    for i in range(2):
        pair_copy(i).start()

    def arrived(k, i):
        piece = slot(bufs[i], k)
        remote(piece, piece, relay_send.at[0, i], recv_sem.at[k, i], ctx, sub).wait_recv()

    docs_copy.wait()
    q_pos = rows * ctx + prefix_units * unit + lax.broadcasted_iota(jnp.int32, (1, rows), 1)
    end = jnp.int32(0)
    first = jnp.zeros((1, rows), jnp.int32)
    for e in range(ndoc):
        end = end + docs[e]
        first = jnp.maximum(first, jnp.where(q_pos >= end, end, 0))

    wide = min(2, per_group)
    span = wide * rows

    def attend(distance):
        base = (reach - distance) * rows
        k_pos = (
            rows * (ctx - distance)
            + prefix_units * unit
            + lax.broadcasted_iota(jnp.int32, (rows, rows), 0)
        )
        allowed = k_pos >= first
        if distance == 0:
            allowed = allowed & (k_pos <= q_pos)
        bias = jnp.where(allowed, 0.0, NEG_FILL)
        bias = jnp.concatenate([bias] * wide, axis=1)
        blocks = [
            (g, (g * per_group + b * wide) * rows)
            for g in range(groups)
            for b in range(per_group // wide)
        ]

        def weigh(g, at):
            here = pl.ds(at, span)
            keys = k_buf[pl.ds(base, rows), pl.ds(g * HEAD_DIM, HEAD_DIM)]
            scores = lax.dot_general(
                keys,
                q_v[here, :],
                (((1,), (1,)), ((), ())),
                preferred_element_type=jnp.float32,
            )
            scores = scores + bias
            top = jnp.max(scores, axis=0, keepdims=True)
            if distance > 0:
                before = max_v[:, here]
                top = jnp.maximum(top, before)
            weights = jnp.exp2((scores - top) * scale)
            total = jnp.sum(weights, axis=0, keepdims=True)
            shrink = None
            if distance > 0:
                shrink = jnp.exp2((before - top) * scale)
                total = total + sum_v[:, here] * shrink
            if distance < reach:
                max_v[:, here] = top
            return weights, total, shrink

        def add(g, at, weights, total, shrink):
            here = pl.ds(at, span)
            values = v_buf[pl.ds(base, rows), pl.ds(g * HEAD_DIM, HEAD_DIM)]
            update = lax.dot_general(
                values,
                weights.astype(jnp.bfloat16),
                (((0,), (0,)), ((), ())),
                preferred_element_type=jnp.float32,
            )
            if distance > 0:
                update = update + acc_v[:, here] * shrink
            sum_v[:, here] = total
            acc_v[:, here] = update

        if distance < reach:
            for g, at in blocks:
                add(g, at, *weigh(g, at))
            return
        take(distance, (0,))
        for g, at in blocks:
            weights, total, shrink = weigh(g, at)
            inverse = 1.0 / total
            weights = (weights * inverse).astype(jnp.bfloat16)
            before = acc_v[:, pl.ds(at, span)] * (shrink * inverse)
            for w in range(wide):
                here = slice(w * rows, (w + 1) * rows)
                there = pl.ds(at + w * rows, rows)
                part_v[there, :] = weights[:, here].T
                done_v[there, :] = before[:, here].T
        take(distance, (1,))
        for g, at in blocks:
            here = pl.ds(at, span)
            values = v_buf[pl.ds(base, rows), pl.ds(g * HEAD_DIM, HEAD_DIM)]
            update = lax.dot_general(
                part_v[here, :],
                values,
                (((1,), (0,)), ((), ())),
                preferred_element_type=jnp.float32,
            )
            result = (done_v[here, :] + update).astype(out_ref.dtype)
            for w in range(wide):
                out_at = (at // rows + w) * HEAD_DIM
                out_ref[:, pl.ds(out_at, HEAD_DIM)] = result[w * rows : (w + 1) * rows]

    for i in range(2):
        arrived(back + other, i)
        relays(back + other, i, lambda copy: copy.start())
    for copy in q_copies:
        copy.wait()

    attend(0)

    def take(distance, kinds=(0, 1)):
        for r in (sub, other):
            k = back - distance * n_sub + r
            for i in kinds:
                arrived(k, i)
                if distance < reach:
                    relays(k, i, lambda copy: copy.start())

    for distance in range(1, reach + 1):
        if distance < reach:
            take(distance)
        attend(distance)

    for j in range(per_cache):

        @pl.when(offset(j) >= 0)
        def _(j=j):
            for t in range(n_sub):
                for i in range(2):
                    cache_copy(j, t, i).wait_send()

    for i in range(2):
        pair_copy(i).wait_send()
    for k in range(n_sub, back + n_sub):
        for i in range(2):
            relays(k, i, lambda copy: copy.wait_send())


def on_device(queries, stretch_keys, stretch_values, cache_keys, cache_values, doc_lengths):
    n_ctx = lax.axis_size("ctx")
    n_sub = lax.axis_size("sub")
    rows = queries.shape[0]
    unit = stretch_keys.shape[0]
    cols = max(1, stretch_keys.shape[1] // HEAD_DIM // n_sub) * HEAD_DIM
    per_cache = cache_keys.shape[0] // unit
    heads = queries.shape[1] // n_sub // HEAD_DIM
    units = (n_ctx // 2 + 1) * n_sub
    return pl.pallas_call(
        functools.partial(kernel, n_ctx, n_sub),
        out_shape=jax.ShapeDtypeStruct((rows, heads * HEAD_DIM), jnp.bfloat16),
        in_specs=[pl.BlockSpec(memory_space=pltpu.HBM)] * 6,
        out_specs=pl.BlockSpec(memory_space=pltpu.VMEM),
        scratch_shapes=[
            pltpu.VMEM((heads * rows, HEAD_DIM), jnp.bfloat16),
            pltpu.VMEM((units * unit, cols), jnp.bfloat16),
            pltpu.VMEM((units * unit, cols), jnp.bfloat16),
            pltpu.SMEM(doc_lengths.shape, jnp.int32),
            pltpu.VMEM((1, heads * rows), jnp.float32),
            pltpu.VMEM((1, heads * rows), jnp.float32),
            pltpu.VMEM((HEAD_DIM, heads * rows), jnp.float32),
            pltpu.VMEM((heads * rows, rows), jnp.bfloat16),
            pltpu.VMEM((heads * rows, HEAD_DIM), jnp.float32),
            pltpu.SemaphoreType.DMA((heads,)),
            pltpu.SemaphoreType.DMA,
            pltpu.SemaphoreType.DMA((2,)),
            pltpu.SemaphoreType.DMA((2,)),
            pltpu.SemaphoreType.DMA((per_cache, n_sub, 2)),
            pltpu.SemaphoreType.DMA((units, 2)),
            pltpu.SemaphoreType.DMA((units, 2)),
            pltpu.SemaphoreType.REGULAR,
        ],
        compiler_params=pltpu.CompilerParams(collective_id=0, has_side_effects=True, vmem_limit_bytes=16 * 1024 * 1024),
        name="attend",
    )(
        *(
            pltpu.with_memory_space_constraint(array, pltpu.HBM)
            for array in (
                queries,
                stretch_keys,
                stretch_values,
                cache_keys,
                cache_values,
                doc_lengths,
            )
        )
    )


def solution(mesh):
    in_specs = (
        P(("grp", "ctx"), "head"),
        P(("grp", "ctx", "sub"), "head"),
        P(("grp", "ctx", "sub"), "head"),
        P(("grp", "ctx", "sub"), "head"),
        P(("grp", "ctx", "sub"), "head"),
        P("grp"),
    )
    out_specs = P(("grp", "ctx"), ("head", "sub"))
    return jax.shard_map(
        on_device, mesh=mesh, in_specs=in_specs, out_specs=out_specs, check_vma=False
    )
```

```python
import functools

import jax
import jax.numpy as jnp
from jax import lax
from jax.experimental import pallas as pl
from jax.experimental.pallas import tpu as pltpu
from jax.sharding import PartitionSpec as P

HEAD_DIM = 128
NEG_FILL = -1e30
LOG2_E = 1.4426950408889634


def kernel(
    n_ctx,
    n_sub,
    q_hbm,
    sk_hbm,
    sv_hbm,
    ck_hbm,
    cv_hbm,
    docs_hbm,
    out_ref,
    q_v,
    k_buf,
    v_buf,
    docs,
    max_v,
    sum_v,
    acc_v,
    part_v,
    q_sem,
    docs_sem,
    own_sem,
    pair_send,
    cache_send,
    relay_send,
    recv_sem,
    pair_sem,
):
    ctx = lax.axis_index("ctx")
    sub = lax.axis_index("sub")
    other = n_sub - 1 - sub
    flat = ctx * n_sub + sub
    rows = q_hbm.shape[0]
    unit = sk_hbm.shape[0]
    all_groups = sk_hbm.shape[1] // HEAD_DIM
    groups = max(1, all_groups // n_sub)
    cols = groups * HEAD_DIM
    heads = q_hbm.shape[1] // HEAD_DIM // n_sub
    per_group = heads // groups
    per_cache = ck_hbm.shape[0] // unit
    prefix_units = per_cache * n_sub * n_ctx
    reach = n_ctx // 2
    back = reach * n_sub
    ndoc = docs_hbm.shape[0]
    scale = HEAD_DIM**-0.5 * LOG2_E

    def remote(src, dst, send, recv, to_ctx, to_sub):
        return pltpu.make_async_remote_copy(
            src_ref=src,
            dst_ref=dst,
            send_sem=send,
            recv_sem=recv,
            device_id={"ctx": to_ctx, "sub": to_sub},
            device_id_type=pl.DeviceIdType.MESH,
        )

    def slot(buf, k):
        start = k * unit
        if not isinstance(k, int):
            start = pl.multiple_of(start, unit)
        return buf.at[pl.ds(start, unit), :]

    def columns(to_sub):
        start = to_sub * all_groups // n_sub * HEAD_DIM
        if not isinstance(start, int):
            start = pl.multiple_of(start, HEAD_DIM)
        return pl.ds(start, cols)

    bufs = (k_buf, v_buf)
    stretch = (sk_hbm, sv_hbm)
    cache = (ck_hbm, cv_hbm)

    barrier = pltpu.get_barrier_semaphore()

    def greet(to_ctx, to_sub):
        pl.semaphore_signal(
            barrier,
            inc=1,
            device_id={"ctx": to_ctx, "sub": to_sub},
            device_id_type=pl.DeviceIdType.MESH,
        )

    first_owner = (prefix_units - back) // (per_cache * n_sub)

    @pl.when(ctx == 0)
    def _():
        for source in range(first_owner, n_ctx):
            greet(source, sub)

    @pl.when(ctx >= 1)
    def _():
        greet(ctx - 1, sub)

    docs_copy = pltpu.make_async_copy(docs_hbm, docs, docs_sem)
    q_copies = []
    for h in range(heads):
        at = pl.multiple_of((sub * heads + h) * HEAD_DIM, HEAD_DIM)
        q_copies.append(
            pltpu.make_async_copy(
                q_hbm.at[:, pl.ds(at, HEAD_DIM)],
                q_v.at[pl.ds(h * rows, rows), :],
                q_sem.at[h],
            )
        )
    own_copies = [
        pltpu.make_async_copy(
            stretch[i].at[:, columns(sub)],
            slot(bufs[i], back + sub),
            own_sem.at[i],
        )
        for i in range(2)
    ]

    def fetch():
        for copy in [*own_copies, docs_copy, *q_copies]:
            copy.start()

    @pl.when(ctx < first_owner)
    def _():
        fetch()

    def offset(j):
        return flat * per_cache + j - (prefix_units - back)

    expected = (
        jnp.where(ctx + 1 < n_ctx, 1, 0)
        + jnp.where(ctx >= first_owner, 1, 0)
        + jnp.where(sub == 0, 1, 0)
    )
    pl.semaphore_wait(barrier, expected)

    @pl.when(sub == 1)
    def _():
        greet(ctx, 0)

    @pl.when(sub == 0)
    def _():
        pl.semaphore_signal(
            pair_sem,
            inc=1,
            device_id={"ctx": ctx, "sub": 1},
            device_id_type=pl.DeviceIdType.MESH,
        )

    def cache_copy(j, t, i):
        to_slot = offset(j)
        return remote(
            cache[i].at[pl.ds(j * unit, unit), columns(t)],
            slot(bufs[i], to_slot),
            cache_send.at[j, t, i],
            recv_sem.at[to_slot, i],
            0,
            t,
        )

    def pair_copy(i):
        return remote(
            stretch[i].at[:, columns(other)],
            slot(bufs[i], back + sub),
            pair_send.at[i],
            recv_sem.at[back + sub, i],
            ctx,
            other,
        )

    def relays(k, i, act):
        @pl.when(ctx + 1 < n_ctx)
        def _():
            act(
                remote(
                    slot(bufs[i], k),
                    slot(bufs[i], k - n_sub),
                    relay_send.at[k, i],
                    recv_sem.at[k - n_sub, i],
                    ctx + 1,
                    sub,
                )
            )

    def send_cache(j, t):
        for i in range(2):
            cache_copy(j, t, i).start()

    @pl.when(sub == 1)
    def _():
        for j in reversed(range(per_cache)):

            @pl.when(offset(j) >= n_sub)
            def _(j=j):
                send_cache(j, 1)

    @pl.when(ctx >= first_owner)
    def _():
        fetch()

    for i in range(2):
        own_copies[i].wait()
        relays(back + sub, i, lambda copy: copy.start())

    @pl.when(sub == 1)
    def _():
        pl.semaphore_wait(pair_sem, 1)

    for j in range(per_cache):

        @pl.when(offset(j) >= n_sub)
        def _(j=j):
            send_cache(j, 0)

            @pl.when(sub == 0)
            def _():
                send_cache(j, 1)

    for j in range(per_cache):

        @pl.when((offset(j) >= 0) & (offset(j) < n_sub))
        def _(j=j):
            for t in range(n_sub):
                send_cache(j, t)

    for i in range(2):
        pair_copy(i).start()

    def arrived(k, i):
        piece = slot(bufs[i], k)
        remote(piece, piece, relay_send.at[0, i], recv_sem.at[k, i], ctx, sub).wait_recv()

    docs_copy.wait()
    q_pos = rows * ctx + prefix_units * unit + lax.broadcasted_iota(jnp.int32, (1, rows), 1)
    end = jnp.int32(0)
    first = jnp.zeros((1, rows), jnp.int32)
    for e in range(ndoc):
        end = end + docs[e]
        first = jnp.maximum(first, jnp.where(q_pos >= end, end, 0))

    wide = min(2, per_group)
    span = wide * rows

    def attend(distance):
        base = (reach - distance) * rows
        k_pos = (
            rows * (ctx - distance)
            + prefix_units * unit
            + lax.broadcasted_iota(jnp.int32, (rows, rows), 0)
        )
        allowed = k_pos >= first
        if distance == 0:
            allowed = allowed & (k_pos <= q_pos)
        bias = jnp.where(allowed, 0.0, NEG_FILL)
        bias = jnp.concatenate([bias] * wide, axis=1)
        blocks = [
            (g, (g * per_group + b * wide) * rows)
            for g in range(groups)
            for b in range(per_group // wide)
        ]

        def weigh(g, at):
            here = pl.ds(at, span)
            keys = k_buf[pl.ds(base, rows), pl.ds(g * HEAD_DIM, HEAD_DIM)]
            scores = lax.dot_general(
                keys,
                q_v[here, :],
                (((1,), (1,)), ((), ())),
                preferred_element_type=jnp.float32,
            )
            scores = scores + bias
            top = jnp.max(scores, axis=0, keepdims=True)
            if distance > 0:
                before = max_v[:, here]
                top = jnp.maximum(top, before)
            weights = jnp.exp2((scores - top) * scale)
            total = jnp.sum(weights, axis=0, keepdims=True)
            shrink = None
            if distance > 0:
                shrink = jnp.exp2((before - top) * scale)
                total = total + sum_v[:, here] * shrink
            if distance < reach:
                max_v[:, here] = top
            return weights.astype(jnp.bfloat16), total, shrink

        def add(g, at, weights, total, shrink):
            here = pl.ds(at, span)
            values = v_buf[pl.ds(base, rows), pl.ds(g * HEAD_DIM, HEAD_DIM)]
            update = lax.dot_general(
                values,
                weights,
                (((0,), (0,)), ((), ())),
                preferred_element_type=jnp.float32,
            )
            if 0 < distance < reach:
                update = update + acc_v[:, here] * shrink
            if distance < reach:
                sum_v[:, here] = total
                acc_v[:, here] = update
            else:
                result = (acc_v[:, here] + update * total).astype(out_ref.dtype)
                for w in range(wide):
                    piece = result[:, w * rows : (w + 1) * rows]
                    out_at = (at // rows + w) * HEAD_DIM
                    out_ref[:, pl.ds(out_at, HEAD_DIM)] = piece.T

        if distance < reach:
            for g, at in blocks:
                add(g, at, *weigh(g, at))
            return
        take(distance, (0,))
        for g, at in blocks:
            weights, total, shrink = weigh(g, at)
            here = pl.ds(at, span)
            part_v[:, here] = weights
            inverse = 1.0 / total
            sum_v[:, here] = inverse
            acc_v[:, here] = acc_v[:, here] * (shrink * inverse)
        take(distance, (1,))
        for g, at in blocks:
            here = pl.ds(at, span)
            add(g, at, part_v[:, here], sum_v[:, here], None)

    for i in range(2):
        arrived(back + other, i)
        relays(back + other, i, lambda copy: copy.start())
    for copy in q_copies:
        copy.wait()

    attend(0)

    def take(distance, kinds=(0, 1)):
        for r in (sub, other):
            k = back - distance * n_sub + r
            for i in kinds:
                arrived(k, i)
                if distance < reach:
                    relays(k, i, lambda copy: copy.start())

    for distance in range(1, reach + 1):
        if distance < reach:
            take(distance)
        attend(distance)

    for j in range(per_cache):

        @pl.when(offset(j) >= 0)
        def _(j=j):
            for t in range(n_sub):
                for i in range(2):
                    cache_copy(j, t, i).wait_send()

    for i in range(2):
        pair_copy(i).wait_send()
    for k in range(n_sub, back + n_sub):
        for i in range(2):
            relays(k, i, lambda copy: copy.wait_send())


def on_device(queries, stretch_keys, stretch_values, cache_keys, cache_values, doc_lengths):
    n_ctx = lax.axis_size("ctx")
    n_sub = lax.axis_size("sub")
    rows = queries.shape[0]
    unit = stretch_keys.shape[0]
    cols = max(1, stretch_keys.shape[1] // HEAD_DIM // n_sub) * HEAD_DIM
    per_cache = cache_keys.shape[0] // unit
    heads = queries.shape[1] // n_sub // HEAD_DIM
    units = (n_ctx // 2 + 1) * n_sub
    return pl.pallas_call(
        functools.partial(kernel, n_ctx, n_sub),
        out_shape=jax.ShapeDtypeStruct((rows, heads * HEAD_DIM), jnp.bfloat16),
        in_specs=[pl.BlockSpec(memory_space=pltpu.HBM)] * 6,
        out_specs=pl.BlockSpec(memory_space=pltpu.VMEM),
        scratch_shapes=[
            pltpu.VMEM((heads * rows, HEAD_DIM), jnp.bfloat16),
            pltpu.VMEM((units * unit, cols), jnp.bfloat16),
            pltpu.VMEM((units * unit, cols), jnp.bfloat16),
            pltpu.SMEM(doc_lengths.shape, jnp.int32),
            pltpu.VMEM((1, heads * rows), jnp.float32),
            pltpu.VMEM((1, heads * rows), jnp.float32),
            pltpu.VMEM((HEAD_DIM, heads * rows), jnp.float32),
            pltpu.VMEM((rows, heads * rows), jnp.bfloat16),
            pltpu.SemaphoreType.DMA((heads,)),
            pltpu.SemaphoreType.DMA,
            pltpu.SemaphoreType.DMA((2,)),
            pltpu.SemaphoreType.DMA((2,)),
            pltpu.SemaphoreType.DMA((per_cache, n_sub, 2)),
            pltpu.SemaphoreType.DMA((units, 2)),
            pltpu.SemaphoreType.DMA((units, 2)),
            pltpu.SemaphoreType.REGULAR,
        ],
        compiler_params=pltpu.CompilerParams(collective_id=0, has_side_effects=True, vmem_limit_bytes=16 * 1024 * 1024),
        name="attend",
    )(
        *(
            pltpu.with_memory_space_constraint(array, pltpu.HBM)
            for array in (
                queries,
                stretch_keys,
                stretch_values,
                cache_keys,
                cache_values,
                doc_lengths,
            )
        )
    )


def solution(mesh):
    in_specs = (
        P(("grp", "ctx"), "head"),
        P(("grp", "ctx", "sub"), "head"),
        P(("grp", "ctx", "sub"), "head"),
        P(("grp", "ctx", "sub"), "head"),
        P(("grp", "ctx", "sub"), "head"),
        P("grp"),
    )
    out_specs = P(("grp", "ctx"), ("head", "sub"))
    return jax.shard_map(
        on_device, mesh=mesh, in_specs=in_specs, out_specs=out_specs, check_vma=False
    )
```

```python
import functools

import jax
import jax.numpy as jnp
from jax import lax
from jax.experimental import pallas as pl
from jax.experimental.pallas import tpu as pltpu
from jax.sharding import PartitionSpec as P

HEAD_DIM = 128
NEG_FILL = -1e30
LOG2_E = 1.4426950408889634


def kernel(
    n_ctx,
    n_sub,
    q_hbm,
    sk_hbm,
    sv_hbm,
    ck_hbm,
    cv_hbm,
    docs_hbm,
    out_ref,
    q_v,
    k_buf,
    v_buf,
    docs,
    max_v,
    sum_v,
    acc_v,
    part_v,
    shrink_v,
    q_sem,
    docs_sem,
    own_sem,
    pair_send,
    cache_send,
    skip_send,
    relay_send,
    recv_sem,
    pair_sem,
):
    ctx = lax.axis_index("ctx")
    sub = lax.axis_index("sub")
    other = n_sub - 1 - sub
    flat = ctx * n_sub + sub
    rows = q_hbm.shape[0]
    unit = sk_hbm.shape[0]
    all_groups = sk_hbm.shape[1] // HEAD_DIM
    groups = max(1, all_groups // n_sub)
    cols = groups * HEAD_DIM
    heads = q_hbm.shape[1] // HEAD_DIM // n_sub
    per_group = heads // groups
    per_cache = ck_hbm.shape[0] // unit
    prefix_units = per_cache * n_sub * n_ctx
    reach = n_ctx // 2
    back = reach * n_sub
    ndoc = docs_hbm.shape[0]
    scale = HEAD_DIM**-0.5 * LOG2_E

    def remote(src, dst, send, recv, to_ctx, to_sub):
        return pltpu.make_async_remote_copy(
            src_ref=src,
            dst_ref=dst,
            send_sem=send,
            recv_sem=recv,
            device_id={"ctx": to_ctx, "sub": to_sub},
            device_id_type=pl.DeviceIdType.MESH,
        )

    def slot(buf, k):
        start = k * unit
        if not isinstance(k, int):
            start = pl.multiple_of(start, unit)
        return buf.at[pl.ds(start, unit), :]

    def columns(to_sub):
        start = to_sub * all_groups // n_sub * HEAD_DIM
        if not isinstance(start, int):
            start = pl.multiple_of(start, HEAD_DIM)
        return pl.ds(start, cols)

    bufs = (k_buf, v_buf)
    stretch = (sk_hbm, sv_hbm)
    cache = (ck_hbm, cv_hbm)

    barrier = pltpu.get_barrier_semaphore()

    def greet(to_ctx, to_sub):
        pl.semaphore_signal(
            barrier,
            inc=1,
            device_id={"ctx": to_ctx, "sub": to_sub},
            device_id_type=pl.DeviceIdType.MESH,
        )

    first_owner = (prefix_units - back) // (per_cache * n_sub)

    @pl.when(ctx == 0)
    def _():
        for source in range(first_owner, n_ctx):
            greet(source, sub)

    @pl.when(ctx == 1)
    def _():
        for source in range(first_owner, n_ctx):
            greet(source, sub)

    @pl.when(ctx >= 1)
    def _():
        greet(ctx - 1, sub)

    docs_copy = pltpu.make_async_copy(docs_hbm, docs, docs_sem)
    q_copies = []
    for h in range(heads):
        at = pl.multiple_of((sub * heads + h) * HEAD_DIM, HEAD_DIM)
        q_copies.append(
            pltpu.make_async_copy(
                q_hbm.at[:, pl.ds(at, HEAD_DIM)],
                q_v.at[pl.ds(h * rows, rows), :],
                q_sem.at[h],
            )
        )
    own_copies = [
        pltpu.make_async_copy(
            stretch[i].at[:, columns(sub)],
            slot(bufs[i], back + sub),
            own_sem.at[i],
        )
        for i in range(2)
    ]

    def fetch():
        for copy in [*own_copies, docs_copy, *q_copies]:
            copy.start()

    @pl.when(ctx < first_owner)
    def _():
        fetch()

    def offset(j):
        return flat * per_cache + j - (prefix_units - back)

    expected = (
        jnp.where(ctx + 1 < n_ctx, 1, 0)
        + jnp.where(ctx >= first_owner, 2, 0)
        + jnp.where(sub == 0, 1, 0)
    )
    pl.semaphore_wait(barrier, expected)

    @pl.when(sub == 1)
    def _():
        greet(ctx, 0)

    @pl.when(sub == 0)
    def _():
        pl.semaphore_signal(
            pair_sem,
            inc=1,
            device_id={"ctx": ctx, "sub": 1},
            device_id_type=pl.DeviceIdType.MESH,
        )

    def cache_copy(j, t, i):
        to_slot = offset(j)
        return remote(
            cache[i].at[pl.ds(j * unit, unit), columns(t)],
            slot(bufs[i], to_slot),
            cache_send.at[j, t, i],
            recv_sem.at[to_slot, i],
            0,
            t,
        )

    def skip_copy(j, t):
        to_slot = offset(j) - n_sub
        return remote(
            cache[1].at[pl.ds(j * unit, unit), columns(t)],
            slot(v_buf, to_slot),
            skip_send.at[j, t],
            recv_sem.at[to_slot, 1],
            1,
            t,
        )

    def pair_copy(i):
        return remote(
            stretch[i].at[:, columns(other)],
            slot(bufs[i], back + sub),
            pair_send.at[i],
            recv_sem.at[back + sub, i],
            ctx,
            other,
        )

    def relays(k, i, act, cached=False):
        skips = (ctx == 0) & (cached and i == 1)

        @pl.when((ctx + 1 < n_ctx) & jnp.logical_not(skips))
        def _():
            act(
                remote(
                    slot(bufs[i], k),
                    slot(bufs[i], k - n_sub),
                    relay_send.at[k, i],
                    recv_sem.at[k - n_sub, i],
                    ctx + 1,
                    sub,
                )
            )

    def send_cache(j, t):
        for i in range(2):
            cache_copy(j, t, i).start()

    @pl.when(sub == 1)
    def _():
        for j in reversed(range(per_cache)):

            @pl.when(offset(j) >= 0)
            def _(j=j):
                cache_copy(j, 1, 0).start()

    @pl.when(ctx >= first_owner)
    def _():
        fetch()

    for i in range(2):
        own_copies[i].wait()
        relays(back + sub, i, lambda copy: copy.start())

    @pl.when(sub == 1)
    def _():
        pl.semaphore_wait(pair_sem, 1)

    for i in range(2):
        for j in (*range(1, per_cache), 0):

            @pl.when(offset(j) >= 0)
            def _(j=j, i=i):
                cache_copy(j, 0, i).start()

        for j in reversed(range(per_cache)):

            @pl.when((offset(j) >= 0) & ((sub == 0) | (i == 1)))
            def _(j=j, i=i):
                cache_copy(j, 1, i).start()

    for i in range(2):
        pair_copy(i).start()
    for i in range(2):
        for j in range(per_cache):

            @pl.when(offset(j) >= n_sub)
            def _(j=j, i=i):
                skip_copy(j, i).start()


    def arrived(k, i):
        piece = slot(bufs[i], k)
        remote(piece, piece, relay_send.at[0, i], recv_sem.at[k, i], ctx, sub).wait_recv()

    docs_copy.wait()
    q_pos = rows * ctx + prefix_units * unit + lax.broadcasted_iota(jnp.int32, (1, rows), 1)
    end = jnp.int32(0)
    first = jnp.zeros((1, rows), jnp.int32)
    for e in range(ndoc):
        end = end + docs[e]
        first = jnp.maximum(first, jnp.where(q_pos >= end, end, 0))

    wide = min(2, per_group)
    span = wide * rows

    blocks = [
        (g, (g * per_group + b * wide) * rows)
        for g in range(groups)
        for b in range(per_group // wide)
    ]

    def mask(distance):
        k_pos = (
            rows * (ctx - distance)
            + prefix_units * unit
            + lax.broadcasted_iota(jnp.int32, (rows, rows), 0)
        )
        allowed = k_pos >= first
        if distance == 0:
            allowed = allowed & (k_pos <= q_pos)
        bias = jnp.where(allowed, 0.0, NEG_FILL)
        return jnp.concatenate([bias] * wide, axis=1)

    def weigh(distance, bias, g, at):
        here = pl.ds(at, span)
        keys = k_buf[pl.ds((reach - distance) * rows, rows), pl.ds(g * HEAD_DIM, HEAD_DIM)]
        scores = lax.dot_general(
            keys,
            q_v[here, :],
            (((1,), (1,)), ((), ())),
            preferred_element_type=jnp.float32,
        )
        scores = scores + bias
        top = jnp.max(scores, axis=0, keepdims=True)
        if distance > 0:
            before = max_v[:, here]
            top = jnp.maximum(top, before)
        weights = jnp.exp2((scores - top) * scale)
        total = jnp.sum(weights, axis=0, keepdims=True)
        shrink = None
        if distance > 0:
            shrink = jnp.exp2((before - top) * scale)
            total = total + sum_v[:, here] * shrink
        if distance < reach:
            max_v[:, here] = top
            sum_v[:, here] = total
        return weights.astype(jnp.bfloat16), total, shrink

    def weighted(distance, g, weights):
        values = v_buf[pl.ds((reach - distance) * rows, rows), pl.ds(g * HEAD_DIM, HEAD_DIM)]
        return lax.dot_general(
            values,
            weights,
            (((0,), (0,)), ((), ())),
            preferred_element_type=jnp.float32,
        )

    def attend(distance):
        bias = mask(distance)
        for g, at in blocks:
            here = pl.ds(at, span)
            weights, _, shrink = weigh(distance, bias, g, at)
            update = weighted(distance, g, weights)
            if distance > 0:
                update = update + acc_v[:, here] * shrink
            acc_v[:, here] = update

    def weigh_all(distance):
        p = distance - (reach - 1)
        bias = mask(distance)
        for g, at in blocks:
            here = pl.ds(at, span)
            weights, total, shrink = weigh(distance, bias, g, at)
            part_v[pl.ds(p * rows, rows), here] = weights
            if p == 0:
                shrink_v[0:1, here] = shrink
            else:
                inverse = 1.0 / total
                sum_v[:, here] = inverse
                shrink_v[1:2, here] = shrink * inverse

    def add_all(distance):
        p = distance - (reach - 1)
        for g, at in blocks:
            here = pl.ds(at, span)
            update = weighted(distance, g, part_v[pl.ds(p * rows, rows), here])
            if p == 0:
                update = update + acc_v[:, here] * shrink_v[0:1, here]
                acc_v[:, here] = update * shrink_v[1:2, here]
            else:
                result = (acc_v[:, here] + update * sum_v[:, here]).astype(out_ref.dtype)
                for w in range(wide):
                    piece = result[:, w * rows : (w + 1) * rows]
                    out_at = (at // rows + w) * HEAD_DIM
                    out_ref[:, pl.ds(out_at, HEAD_DIM)] = piece.T

    for i in range(2):
        arrived(back + other, i)
        relays(back + other, i, lambda copy: copy.start())
    for copy in q_copies:
        copy.wait()

    attend(0)

    def take(distance, kinds=(0, 1)):
        for r in (sub, other):
            k = back - distance * n_sub + r
            for i in kinds:
                arrived(k, i)
                if distance < reach:
                    relays(k, i, lambda copy: copy.start(), True)

    for distance in range(1, reach - 1):
        take(distance)
        attend(distance)
    take(reach - 1, (0,))

    @pl.when(ctx > 0)
    def _():
        take(reach - 1, (1,))

    weigh_all(reach - 1)
    take(reach, (0,))
    weigh_all(reach)

    @pl.when(ctx == 0)
    def _():
        take(reach - 1, (1,))

    add_all(reach - 1)
    take(reach, (1,))
    add_all(reach)

    for j in range(per_cache):

        @pl.when(offset(j) >= 0)
        def _(j=j):
            for t in range(n_sub):
                for i in range(2):
                    cache_copy(j, t, i).wait_send()

    for i in range(2):
        for j in range(per_cache):

            @pl.when(offset(j) >= n_sub)
            def _(j=j, i=i):
                skip_copy(j, i).wait_send()

    for i in range(2):
        pair_copy(i).wait_send()
    for k in range(n_sub, back + n_sub):
        for i in range(2):
            relays(k, i, lambda copy: copy.wait_send(), k < back)


def on_device(queries, stretch_keys, stretch_values, cache_keys, cache_values, doc_lengths):
    n_ctx = lax.axis_size("ctx")
    n_sub = lax.axis_size("sub")
    rows = queries.shape[0]
    unit = stretch_keys.shape[0]
    cols = max(1, stretch_keys.shape[1] // HEAD_DIM // n_sub) * HEAD_DIM
    per_cache = cache_keys.shape[0] // unit
    heads = queries.shape[1] // n_sub // HEAD_DIM
    units = (n_ctx // 2 + 1) * n_sub
    return pl.pallas_call(
        functools.partial(kernel, n_ctx, n_sub),
        out_shape=jax.ShapeDtypeStruct((rows, heads * HEAD_DIM), jnp.bfloat16),
        in_specs=[pl.BlockSpec(memory_space=pltpu.HBM)] * 6,
        out_specs=pl.BlockSpec(memory_space=pltpu.VMEM),
        scratch_shapes=[
            pltpu.VMEM((heads * rows, HEAD_DIM), jnp.bfloat16),
            pltpu.VMEM((units * unit, cols), jnp.bfloat16),
            pltpu.VMEM((units * unit, cols), jnp.bfloat16),
            pltpu.SMEM(doc_lengths.shape, jnp.int32),
            pltpu.VMEM((1, heads * rows), jnp.float32),
            pltpu.VMEM((1, heads * rows), jnp.float32),
            pltpu.VMEM((HEAD_DIM, heads * rows), jnp.float32),
            pltpu.VMEM((2 * rows, heads * rows), jnp.bfloat16),
            pltpu.VMEM((2, heads * rows), jnp.float32),
            pltpu.SemaphoreType.DMA((heads,)),
            pltpu.SemaphoreType.DMA,
            pltpu.SemaphoreType.DMA((2,)),
            pltpu.SemaphoreType.DMA((2,)),
            pltpu.SemaphoreType.DMA((per_cache, n_sub, 2)),
            pltpu.SemaphoreType.DMA((per_cache, n_sub)),
            pltpu.SemaphoreType.DMA((units, 2)),
            pltpu.SemaphoreType.DMA((units, 2)),
            pltpu.SemaphoreType.REGULAR,
        ],
        compiler_params=pltpu.CompilerParams(collective_id=0, has_side_effects=True, vmem_limit_bytes=16 * 1024 * 1024),
        name="attend",
    )(
        *(
            pltpu.with_memory_space_constraint(array, pltpu.HBM)
            for array in (
                queries,
                stretch_keys,
                stretch_values,
                cache_keys,
                cache_values,
                doc_lengths,
            )
        )
    )


def solution(mesh):
    in_specs = (
        P(("grp", "ctx"), "head"),
        P(("grp", "ctx", "sub"), "head"),
        P(("grp", "ctx", "sub"), "head"),
        P(("grp", "ctx", "sub"), "head"),
        P(("grp", "ctx", "sub"), "head"),
        P("grp"),
    )
    out_specs = P(("grp", "ctx"), ("head", "sub"))
    return jax.shard_map(
        on_device, mesh=mesh, in_specs=in_specs, out_specs=out_specs, check_vma=False
    )
```
